128 devices in a mesh: kxy: 16 (over z_lo, y, core), kz: 8 (over z_hi, x).
Axes of the slice: x: 4, y: 4, z: 4 (z_hi: 2, z_lo: 2; z = z_hi * 2 + z_lo), core: 2. Of those that a mesh axis runs over, the one named last changes fastest.
Arguments:
- factors: float32 [16, 8, 2, 384, 1024], P('kxy', 'kz'), may hold values from -0.9 to 0.9
- occ_energy: float32 [16, 8, 8], P('kxy', 'kz'), may hold values from -2 to -0.5
- vir_energy: float32 [16, 8, 128], P('kxy', 'kz'), may hold values from 0.5 to 3
- shifts: int32 [2, 2], replicated, may hold values from 0 to 3, as said below
Outputs:
- gradient: float32 [16, 8, 2, 384, 1024], P('kxy', 'kz')
The draws below stay inside these ranges and needn't reach their ends.
Inputs may be any that keep to these rules, and one draw needn't show every extreme that they name: `shifts`: row 0 (the momentum transfer) has both entries between 1 and 3. Row 1 is the partner displacement; it is always (3, 3).
All inputs are finite; a program needn't handle non-finite values.
Results may differ from the reference program's by a relative error of at most 0.0001.
Values sent between devices are 32-bit elements; how exact they have to be, the bound alone decides.
No kernel may reach another device: no remote copies, remote signals or barrier semaphores. Data moves between devices by JAX's collectives and lax.ppermute only.
A program may use at most 64 MiB of HBM per device.

```python
import jax
import jax.numpy as jnp
from jax import lax

NO = 8
NV = 128
NAUX = 384
REACH = 4
NDISP = 1
NKX = 16
NKZ = 8


def draw_shifts(key, part):
    subkeys = jax.random.split(jax.random.fold_in(key, 17), 4)
    transfer = 1 + jax.random.randint(subkeys[0], (1, 2), 0, REACH - 1)
    displaced = jax.random.randint(subkeys[1], (NDISP, 2), 0, REACH)
    row_first = jax.random.randint(subkeys[2], (), 0, NDISP)
    row_third = jax.random.randint(subkeys[3], (), 0, NDISP)
    displaced = displaced.at[row_first, 0].set(REACH - 1)
    displaced = displaced.at[row_third, 1].set(REACH - 1)
    return jnp.concatenate([transfer, displaced], 0).astype(jnp.int32)


def shard_levels(key, shape, pieces, low, top_value):
    def one(axis_at, blocks):
        draws = jax.random.uniform(jax.random.fold_in(jax.random.fold_in(key, 6), axis_at), (blocks,), jnp.float32, low / len(pieces), top_value / len(pieces))
        return jnp.repeat(jnp.exp(draws), shape[axis_at] // blocks).reshape((-1,) + (1,) * (len(shape) - axis_at - 1))

    loudness = one(*pieces[0])
    for cut in pieces[1:]:
        loudness = loudness * one(*cut)
    return loudness


def noise(own_key, extent, deviation, bound, cuts=(), kind=jnp.bfloat16):
    array = jax.random.normal(own_key, extent, jnp.float32) * deviation
    if len(cuts) > 0:
        array = shard_levels(own_key, extent, cuts, -0.22, 0.18) * array
    return jnp.clip(array, min=-bound, max=bound).astype(kind)


def setup_inputs(seed: int = 0) -> dict:
    key_of = jax.random.split(jax.random.key(seed), 5)
    factors = noise(key_of[0], (NKX, NKZ, 2, NAUX, NO * NV), 0.15, 0.9, ((0, 16), (1, 8)), jnp.float32)
    occ_energy = jnp.clip(-2.0 + 1.5 * jax.random.uniform(key_of[1], (NKX, NKZ, NO), jnp.float32) ** shard_levels(key_of[1], (NKX, NKZ, NO), ((0, 16), (1, 8)), -0.2, 0.2), -2.0, -0.5)
    vir_energy = jnp.clip(0.5 + 2.5 * jax.random.uniform(key_of[2], (NKX, NKZ, NV), jnp.float32) ** shard_levels(key_of[2], (NKX, NKZ, NV), ((0, 16), (1, 8)), -0.2, 0.2), 0.5, 3.0)
    shifts = draw_shifts(jax.random.fold_in(key_of[4], 71), 0)
    return {"factors": factors, "occ_energy": occ_energy, "vir_energy": vir_energy, "shifts": shifts}


def product(left, right):
    return jnp.dot(left, right, precision=lax.Precision.HIGHEST, preferred_element_type=jnp.float32)


def pair_terms(payload):
    own_panel, partner, occ_own, vir_own, occ_part, vir_part = payload
    own_re, own_im = own_panel[0], own_panel[1]
    part_re, part_im = partner[0], partner[1]
    real_v = product(own_re.T, part_re) + product(own_im.T, part_im)
    imag_v = product(own_im.T, part_re) - product(own_re.T, part_im)
    gap_own = (vir_own[None, :] - occ_own[:, None]).reshape(-1)
    gap_part = (vir_part[None, :] - occ_part[:, None]).reshape(-1)
    denominator = gap_own[:, None] + gap_part[None, :]
    real_t = real_v / denominator
    imag_t = imag_v / denominator
    own_grad = jnp.stack([product(part_re, real_t.T) - product(part_im, imag_t.T),
                          product(part_re, imag_t.T) + product(part_im, real_t.T)])
    part_grad = jnp.stack([product(own_re, real_t) + product(own_im, imag_t),
                           product(own_im, real_t) - product(own_re, imag_t)])
    return own_grad, part_grad


def reference(factors, occ_energy, vir_energy, shifts):
    kx_count, kz_count = factors.shape[0], factors.shape[1]
    count = kx_count * kz_count
    vir_used = jnp.roll(vir_energy, (-shifts[0, 0], -shifts[0, 1]), (0, 1))
    gradient_sum = jnp.zeros(factors.shape, jnp.float32)
    flat_panel = factors.reshape((count,) + factors.shape[2:])
    flat_occ = occ_energy.reshape(count, -1)
    flat_vir = vir_used.reshape(count, -1)
    for which_pair in range(NDISP):
        step_x = shifts[which_pair + 1, 0]
        step_z = shifts[which_pair + 1, 1]
        partner = jnp.roll(factors, (-step_x, -step_z), (0, 1)).reshape(flat_panel.shape)
        occ_part = jnp.roll(occ_energy, (-step_x, -step_z), (0, 1)).reshape(flat_occ.shape)
        vir_part = jnp.roll(vir_used, (-step_x, -step_z), (0, 1)).reshape(flat_vir.shape)
        own_grad, part_grad = lax.map(pair_terms, (flat_panel, partner, flat_occ, flat_vir, occ_part, vir_part))
        own_grad = own_grad.reshape(factors.shape)
        part_grad = part_grad.reshape(factors.shape)
        gradient_sum = gradient_sum + own_grad + jnp.roll(part_grad, (step_x, step_z), (0, 1))
    return -gradient_sum
```

```python
import jax
import jax.numpy as jnp
from jax import lax
from jax.sharding import PartitionSpec as P

REACH = 4
AXES = ("kxy", "kz")
MEET_Z = ((0, 0, 1, 1), (3, 2, 3, 3), (3, 2, 3, 3), (1, 0, 0, 0))


def coordinates(kx, kz):
    return kz % 4, (kx // 2) % 4, 2 * (kz // 4) + kx // 8


def device(x, y, z, core):
    return (8 * (z % 2) + 2 * (y % 4) + core) * 8 + 4 * (z // 2) + x


def routes(count_x, count_z):
    odd, after, before = {}, {}, {}
    for kx in range(1, count_x, 2):
        for kz in range(count_z):
            x, y, z = coordinates(kx, kz)
            meet = (x, y - 1, z ^ MEET_Z[x][y])
            odd[kx * count_z + kz] = meet
            after[(kx + 3) % count_x * count_z + (kz + 3) % count_z] = meet
            before[(kx - 3) % count_x * count_z + (kz - 3) % count_z] = meet
    return odd, after, before


def onto(meets, core):
    return {source: device(*meet, core) for source, meet in meets.items()}


def move(x, route):
    return lax.ppermute(x, AXES, sorted(route.items()))


def move_back(x, route):
    return lax.ppermute(x, AXES, sorted((t, s) for s, t in route.items()))


def shifted(x, axis, by):
    size = lax.axis_size(axis)
    return lax.ppermute(x, axis, [(i, (i + by) % size) for i in range(size)])


def pulled(x, axis, step):
    arrived = [shifted(x, axis, -by) for by in range(1, REACH)]
    return jnp.where(step == 1, arrived[0], jnp.where(step == 2, arrived[1], arrived[2]))


def product(left, right, inner_left, inner_right):
    return lax.dot_general(
        left,
        right,
        (((inner_left,), (inner_right,)), ((), ())),
        precision=lax.Precision.HIGH,
        preferred_element_type=jnp.float32,
    )


def pair(u, w, gap_u, gap_w):
    denominator = gap_u[:, None] + gap_w[None, :]
    real_a = (product(u[0], w[0], 0, 0) + product(u[1], w[1], 0, 0)) / denominator
    imag_a = (product(u[1], w[0], 0, 0) - product(u[0], w[1], 0, 0)) / denominator
    to_u = (
        product(w[0], real_a, 1, 1) - product(w[1], imag_a, 1, 1),
        product(w[0], imag_a, 1, 1) + product(w[1], real_a, 1, 1),
    )
    to_w = (
        product(u[0], real_a, 1, 0) + product(u[1], imag_a, 1, 0),
        product(u[1], real_a, 1, 0) - product(u[0], imag_a, 1, 0),
    )
    return jnp.stack(to_u), jnp.stack(to_w)


def body(factors, occ_energy, vir_energy, shifts):
    count_x, count_z = lax.axis_size("kxy"), lax.axis_size("kz")
    odd, after, before = routes(count_x, count_z)
    route_a = {**onto(odd, 0), **onto(after, 1)}
    route_b = {**onto(odd, 1), **onto(before, 0)}
    route_c = onto(after, 1)
    route_d = onto(before, 0)
    cores = {i: i ^ count_z for i in range(count_x * count_z)}
    upper = lax.axis_index("kxy") % 2 == 1

    own = factors[0, 0]
    half = own.shape[-1] // 2
    first, second = own[..., :half], own[..., half:]
    u_first = move(first, route_a)
    w_second = move(second, route_b)
    u_even = move(second, route_c)
    w_even = move(first, route_d)

    vir = pulled(vir_energy[0, 0], "kxy", shifts[0, 0])
    vir = pulled(vir, "kz", shifts[0, 1])
    gap = (vir[None, :] - occ_energy[0, 0][:, None]).reshape(-1)
    gap_u = move(gap, route_a)
    gap_w = move(gap, route_b)
    u_first, w_second, gap_u, gap_w = lax.optimization_barrier((u_first, w_second, gap_u, gap_w))

    crossed = move(jnp.where(upper, w_second, u_first), cores)
    u = jnp.concatenate([u_first, jnp.where(upper, u_even, crossed)], -1)
    w = jnp.concatenate([jnp.where(upper, crossed, w_even), w_second], -1)

    to_u, to_w = pair(u, w, gap_u, gap_w)

    back_even_second = move_back(to_u[..., half:], route_c)
    back_even_first = move_back(to_w[..., :half], route_d)
    met = move(jnp.where(upper, to_w[..., :half], to_u[..., half:]), cores)
    back_first = move_back(to_u[..., :half] + jnp.where(upper, 0.0, met), route_a)
    back_second = move_back(to_w[..., half:] + jnp.where(upper, met, 0.0), route_b)
    total = jnp.concatenate([back_first + back_even_first, back_second + back_even_second], -1)
    return (-total)[None, None]


def solution(mesh):
    placed = (P("kxy", "kz", None, None, None), P("kxy", "kz", None), P("kxy", "kz", None), P())
    return jax.shard_map(
        body,
        mesh=mesh,
        in_specs=placed,
        out_specs=P("kxy", "kz", None, None, None),
        check_vma=False,
    )
```

```python
import functools

import jax
import jax.numpy as jnp
from jax import lax
from jax.experimental import pallas as pl
from jax.experimental.pallas import tpu as pltpu
from jax.sharding import PartitionSpec as P


REACH = 4
LIMIT = 26 << 20
AXES = ("kxy", "kz")
MEET_Z = ((0, 0, 1, 1), (3, 2, 3, 3), (3, 2, 3, 3), (1, 0, 0, 0))


def coordinates(kx, kz):
    return kz % 4, (kx // 2) % 4, 2 * (kz // 4) + kx // 8


def device(x, y, z, core):
    return (8 * (z % 2) + 2 * (y % 4) + core) * 8 + 4 * (z // 2) + x


def routes(count_x, count_z):
    odd, after, before = {}, {}, {}
    for kx in range(1, count_x, 2):
        for kz in range(count_z):
            x, y, z = coordinates(kx, kz)
            meet = (x, y - 1, z ^ MEET_Z[x][y])
            odd[kx * count_z + kz] = meet
            after[(kx + 3) % count_x * count_z + (kz + 3) % count_z] = meet
            before[(kx - 3) % count_x * count_z + (kz - 3) % count_z] = meet
    return odd, after, before


def onto(meets, core):
    return {source: device(*meet, core) for source, meet in meets.items()}


def move(x, route):
    return lax.ppermute(x, AXES, sorted(route.items()))


def move_back(x, route):
    return lax.ppermute(x, AXES, sorted((t, s) for s, t in route.items()))


def split(x):
    high = x.astype(jnp.bfloat16)
    return high, (x - high.astype(jnp.float32)).astype(jnp.bfloat16)


def left(x, axis):
    high, low = split(x)
    return jnp.concatenate([high, high, low], axis)


def right(x, axis):
    high, low = split(x)
    return jnp.concatenate([high, low, high], axis)


def product(x, y, inner_x, inner_y):
    return lax.dot_general(
        x, y, (((inner_x,), (inner_y,)), ((), ())), preferred_element_type=jnp.float32
    )


def block_kernel(has_o, has_w, *refs):
    o_ref, w_ref, gap_o_ref, gap_w_ref, *refs = refs
    old_o = refs.pop(0) if has_o else None
    old_w = refs.pop(0) if has_w else None
    to_o, to_w, tall, flat = refs
    a, b = o_ref[0], o_ref[1]
    inner = a.shape[0]
    for i, x in enumerate((a, b, a + b)):
        flat[i] = left(x, 1)
        high, low = split(x.T)
        tall[i, :, :inner] = high
        tall[i, :, inner : 2 * inner] = high
        tall[i, :, 2 * inner :] = low
    c, d = w_ref[0], w_ref[1]
    ac = product(tall[0], right(c, 0), 1, 0)
    bd = product(tall[1], right(d, 0), 1, 0)
    both = product(tall[2], right(c - d, 0), 1, 0)
    inverse = 1.0 / (gap_o_ref[...] + gap_w_ref[...])
    p = (ac + bd) * inverse
    q = (both - ac + bd) * inverse
    cp = product(left(c, 1), right(p, 1), 1, 1)
    dq = product(left(d, 1), right(q, 1), 1, 1)
    both = product(left(c + d, 1), right(p + q, 1), 1, 1)
    re, im = cp - dq, both - cp - dq
    to_o[0] = re + old_o[0] if has_o else re
    to_o[1] = im + old_o[1] if has_o else im
    ap = product(flat[0], right(p, 0), 1, 0)
    bq = product(flat[1], right(q, 0), 1, 0)
    both = product(flat[2], right(p - q, 0), 1, 0)
    re, im = ap + bq, both - ap + bq
    to_w[0] = re + old_w[0] if has_w else re
    to_w[1] = im + old_w[1] if has_w else im


def block(o, w, gap_o, gap_w, old_o=None, old_w=None):
    inner, m = o.shape[1:]
    n = w.shape[2]
    old = [x for x in (old_o, old_w) if x is not None]
    spec = pl.BlockSpec(memory_space=pltpu.VMEM)
    return pl.pallas_call(
        functools.partial(block_kernel, old_o is not None, old_w is not None),
        out_shape=(jax.ShapeDtypeStruct(o.shape, jnp.float32), jax.ShapeDtypeStruct(w.shape, jnp.float32)),
        in_specs=[spec] * (4 + len(old)),
        out_specs=(spec, spec),
        scratch_shapes=[
            pltpu.VMEM((3, m, 3 * inner), jnp.bfloat16),
            pltpu.VMEM((3, inner, 3 * m), jnp.bfloat16),
        ],
        compiler_params=pltpu.CompilerParams(vmem_limit_bytes=LIMIT),
        cost_estimate=pl.CostEstimate(
            flops=54 * inner * m * n, bytes_accessed=16 * inner * (m + n), transcendentals=m * n
        ),
    )(o, w, gap_o.reshape(m, 1), gap_w.reshape(1, n), *old)


def moved_from(route, by_x, by_z, count_x, count_z):
    out = {}
    for k, target in route.items():
        kx, kz = divmod(k, count_z)
        out[(kx + by_x) % count_x * count_z + (kz + by_z) % count_z] = target
    return out


def body(factors, occ_energy, vir_energy, shifts):
    count_x, count_z = lax.axis_size("kxy"), lax.axis_size("kz")
    odd, after, before = routes(count_x, count_z)
    route_a = {**onto(odd, 0), **onto(after, 1)}
    route_b = {**onto(odd, 1), **onto(before, 0)}
    route_after = onto(after, 1)
    route_before = onto(before, 0)
    cores = {i: i ^ count_z for i in range(count_x * count_z)}
    upper = lax.axis_index("kxy") % 2 == 1

    own = factors[0, 0]
    half = own.shape[-1] // 2
    first, second = own[..., :half], own[..., half:]
    arrived_a = move(first, route_a)
    arrived_b = move(second, route_b)
    rest_after = move(second, route_after)
    rest_before = move(first, route_before)

    def send_energies(by_x, by_z):
        def send(vir):
            return tuple(
                move(vir, moved_from(route, by_x, by_z, count_x, count_z)) for route in (route_a, route_b)
            )

        return send

    span = REACH - 1
    sends = [send_energies(1 + i // span, 1 + i % span) for i in range(span * span)]
    vir_a, vir_b = lax.switch((shifts[0, 0] - 1) * span + shifts[0, 1] - 1, sends, vir_energy[0, 0])
    occ_a = move(occ_energy[0, 0], route_a)
    occ_b = move(occ_energy[0, 0], route_b)
    gap_a = (vir_a[None, :] - occ_a[:, None]).reshape(2, half)
    gap_b = (vir_b[None, :] - occ_b[:, None]).reshape(2, half)
    gap_o = jnp.where(upper, gap_b[::-1], gap_a)
    gap_w = jnp.where(upper, gap_a, gap_b[::-1])

    o_a = jnp.where(upper, arrived_b, arrived_a)
    w_f = jnp.where(upper, arrived_a, arrived_b)
    o_b = move(o_a, cores)
    w_s = jnp.where(upper, rest_after, rest_before)

    to_a, to_f = block(o_a, w_f, gap_o[0], gap_w[0])
    to_b, to_f = block(o_b, w_f, gap_o[1], gap_w[0], old_w=to_f)
    back_after = move_back(to_f, route_after)
    back_before = move_back(to_f, route_before)
    to_b, to_s = block(o_b, w_s, gap_o[1], gap_w[1], old_o=to_b)
    crossed = move(to_b, cores)
    to_a, to_s = block(o_a, w_s, gap_o[0], gap_w[1], to_a, to_s)
    to_a = to_a + crossed
    back_a = move_back(jnp.where(upper, to_s, to_a), route_a)
    back_b = move_back(jnp.where(upper, to_a, to_s), route_b)
    total = jnp.concatenate(
        [
            back_after + jnp.where(upper, back_a, back_b),
            back_before + jnp.where(upper, back_b, back_a),
        ],
        -1,
    )
    return (-total)[None, None]


def solution(mesh):
    placed = (P("kxy", "kz", None, None, None), P("kxy", "kz", None), P("kxy", "kz", None), P())
    return jax.shard_map(
        body,
        mesh=mesh,
        in_specs=placed,
        out_specs=P("kxy", "kz", None, None, None),
        check_vma=False,
    )
```

```python
import functools

import jax
import jax.numpy as jnp
from jax import lax
from jax.experimental import pallas as pl
from jax.experimental.pallas import tpu as pltpu
from jax.sharding import PartitionSpec as P


REACH = 4
LIMIT = 24 << 20
AXES = ("kxy", "kz")
MEET_Z = ((0, 0, 1, 1), (3, 2, 3, 3), (3, 2, 3, 3), (1, 0, 0, 0))


def coordinates(kx, kz):
    return kz % 4, (kx // 2) % 4, 2 * (kz // 4) + kx // 8


def device(x, y, z, core):
    return (8 * (z % 2) + 2 * (y % 4) + core) * 8 + 4 * (z // 2) + x


def routes(count_x, count_z):
    odd, after, before = {}, {}, {}
    for kx in range(1, count_x, 2):
        for kz in range(count_z):
            x, y, z = coordinates(kx, kz)
            meet = (x, y - 1, z ^ MEET_Z[x][y])
            odd[kx * count_z + kz] = meet
            after[(kx + 3) % count_x * count_z + (kz + 3) % count_z] = meet
            before[(kx - 3) % count_x * count_z + (kz - 3) % count_z] = meet
    return odd, after, before


def onto(meets, core):
    return {source: device(*meet, core) for source, meet in meets.items()}


def move(x, route):
    return lax.ppermute(x, AXES, sorted(route.items()))


def move_back(x, route):
    return lax.ppermute(x, AXES, sorted((t, s) for s, t in route.items()))


def split(x):
    high = x.astype(jnp.bfloat16)
    return high, (x - high.astype(jnp.float32)).astype(jnp.bfloat16)


def left(x, axis):
    high, low = split(x)
    return jnp.concatenate([high, high, low], axis)


def right(x, axis):
    high, low = split(x)
    return jnp.concatenate([high, low, high], axis)


def product(x, y, inner_x, inner_y):
    return lax.dot_general(
        x, y, (((inner_x,), (inner_y,)), ((), ())), preferred_element_type=jnp.float32
    )


def on_upper():
    return lax.axis_index("kxy") % 2 == 1


def block_kernel(has_o, has_w, *refs):
    o_ref, w_ref, gap_o, gap_w, *refs = refs
    old_o = refs.pop(0) if has_o else None
    old_w = refs.pop(0) if has_w else None
    to_o, to_w, tall, flat = refs
    inner = to_o.shape[1]

    a, b = o_ref[0], o_ref[1]
    for i, x in enumerate((a, b, a + b)):
        flat[i] = left(x, 1)
        high, low = split(x.T)
        tall[i, :, :inner] = high
        tall[i, :, inner : 2 * inner] = high
        tall[i, :, 2 * inner :] = low
    c, d = w_ref[0], w_ref[1]
    ac = product(tall[0], right(c, 0), 1, 0)
    bd = product(tall[1], right(d, 0), 1, 0)
    both = product(tall[2], right(c - d, 0), 1, 0)
    inverse = 1.0 / (gap_o[...] + gap_w[...])
    p = (ac + bd) * inverse
    q = (both - ac + bd) * inverse
    cp = product(left(c, 1), right(p, 1), 1, 1)
    dq = product(left(d, 1), right(q, 1), 1, 1)
    both = product(left(c + d, 1), right(p + q, 1), 1, 1)
    re, im = cp - dq, both - cp - dq
    to_o[0] = re + old_o[0] if has_o else re
    to_o[1] = im + old_o[1] if has_o else im
    ap = product(flat[0], right(p, 0), 1, 0)
    bq = product(flat[1], right(q, 0), 1, 0)
    both = product(flat[2], right(p - q, 0), 1, 0)
    re, im = ap + bq, both - ap + bq
    to_w[0] = re + old_w[0] if has_w else re
    to_w[1] = im + old_w[1] if has_w else im


def block(o, w, gap_o, gap_w, old_o=None, old_w=None):
    parts, inner, half = o.shape
    old = [x for x in (old_o, old_w) if x is not None]
    spec = pl.BlockSpec(memory_space=pltpu.VMEM)
    return pl.pallas_call(
        functools.partial(block_kernel, old_o is not None, old_w is not None),
        out_shape=(jax.ShapeDtypeStruct((parts, inner, half), jnp.float32),) * 2,
        in_specs=[spec] * (4 + len(old)),
        out_specs=(spec, spec),
        scratch_shapes=[
            pltpu.VMEM((3, half, 3 * inner), jnp.bfloat16),
            pltpu.VMEM((3, inner, 3 * half), jnp.bfloat16),
        ],
        compiler_params=pltpu.CompilerParams(vmem_limit_bytes=LIMIT),
        cost_estimate=pl.CostEstimate(
            flops=54 * inner * half * half, bytes_accessed=32 * inner * half, transcendentals=half * half
        ),
    )(o, w, gap_o, gap_w, *old)


def moved_from(route, by_x, by_z, count_x, count_z):
    out = {}
    for k, target in route.items():
        kx, kz = divmod(k, count_z)
        out[(kx + by_x) % count_x * count_z + (kz + by_z) % count_z] = target
    return out


def choose_kernel(turned, if_lower, if_upper, first, second, sems):
    half = first.shape[2]
    upper = on_upper()

    def copies(source, turned):
        at = [pl.ds(i * half, half) for i in ((1, 0) if turned else (0, 1))]
        return (
            pltpu.make_async_copy(source.at[:, :, at[0]], first, sems.at[0]),
            pltpu.make_async_copy(source.at[:, :, at[1]], second, sems.at[1]),
        )

    @pl.when(upper)
    def _():
        for copy in copies(if_upper, turned):
            copy.start()

    @pl.when(jnp.logical_not(upper))
    def _():
        for copy in copies(if_lower, False):
            copy.start()

    for copy in copies(if_lower, False):
        copy.wait()


def choose(if_lower, if_upper, turned):
    parts, inner, pairs = if_lower.shape
    spec = pl.BlockSpec(memory_space=pltpu.VMEM)
    return pl.pallas_call(
        functools.partial(choose_kernel, turned),
        out_shape=(jax.ShapeDtypeStruct((parts, inner, pairs // 2), if_lower.dtype),) * 2,
        in_specs=[pl.BlockSpec(memory_space=pl.ANY)] * 2,
        out_specs=(spec, spec),
        scratch_shapes=[pltpu.SemaphoreType.DMA((2,))],
        compiler_params=pltpu.CompilerParams(vmem_limit_bytes=LIMIT),
        cost_estimate=pl.CostEstimate(flops=0, bytes_accessed=8 * if_lower.size, transcendentals=0),
    )(if_lower, if_upper)


def gap_kernel(vir_a, vir_b, occ_a, occ_b, first_o, second_o, first_w, second_w):
    upper = on_upper()
    occ_o = jnp.where(upper, occ_b[...], occ_a[...])
    occ_w = jnp.where(upper, occ_a[...], occ_b[...])
    vir_o = jnp.where(upper, vir_b[...], vir_a[...])
    vir_w = jnp.where(upper, vir_a[...], vir_b[...])
    span = vir_o.shape[1]
    vir_o = jnp.broadcast_to(vir_o, (8, span)).T[:, :1]
    each = first_o.shape[0] // span
    for i in range(each):
        lower_occ, upper_occ = occ_o[:, i : i + 1], occ_o[:, each + i : each + i + 1]
        at = pl.ds(i * span, span)
        first_o[at, :] = vir_o - jnp.where(upper, upper_occ, lower_occ)
        second_o[at, :] = vir_o - jnp.where(upper, lower_occ, upper_occ)
        first_w[:, at] = vir_w - occ_w[:, i : i + 1]
        second_w[:, at] = vir_w - occ_w[:, each + i : each + i + 1]


def gaps(vir_a, vir_b, occ_a, occ_b):
    half = vir_a.shape[1] * occ_a.shape[1] // 2
    spec = pl.BlockSpec(memory_space=pltpu.VMEM)
    column = jax.ShapeDtypeStruct((half, 1), vir_a.dtype)
    row = jax.ShapeDtypeStruct((1, half), vir_a.dtype)
    out = pl.pallas_call(
        gap_kernel,
        out_shape=(column, column, row, row),
        in_specs=[spec] * 4,
        out_specs=(spec,) * 4,
        compiler_params=pltpu.CompilerParams(vmem_limit_bytes=LIMIT),
    )(vir_a, vir_b, occ_a, occ_b)
    return out[:2], out[2:]


def merge_kernel(to_a, met, to_s, for_a, for_b):
    own = to_a[...] + met[...]
    other = to_s[...]
    upper = on_upper()
    for_a[...] = jnp.where(upper, other, own)
    for_b[...] = jnp.where(upper, own, other)


def merge(to_a, met, to_s):
    spec = pl.BlockSpec(memory_space=pltpu.VMEM)
    return pl.pallas_call(
        merge_kernel,
        out_shape=(jax.ShapeDtypeStruct(to_a.shape, to_a.dtype),) * 2,
        in_specs=[spec] * 3,
        out_specs=(spec, spec),
        compiler_params=pltpu.CompilerParams(vmem_limit_bytes=LIMIT),
    )(to_a, met, to_s)


def finish_kernel(early, lowered, back_a, back_b, out, held, sems):
    half = back_a.shape[2]
    steps = sems.shape[0]
    rows = back_a.shape[1] // steps
    upper = on_upper()
    copies = []
    for i in range(steps):
        at = pl.ds(i * rows, rows)
        a, b = back_a[:, at], back_b[:, at]
        held[:, at, :half] = -jnp.where(upper, a, early[:, at] + lowered[:, at])
        held[:, at, half:] = -jnp.where(upper, b, a + b)
        copies.append(pltpu.make_async_copy(held.at[:, at], out.at[:, at], sems.at[i]))
        copies[-1].start()
    for copy in copies:
        copy.wait()


def finish(*backs):
    parts, inner, half = backs[0].shape
    shape = (parts, inner, 2 * half)
    return pl.pallas_call(
        finish_kernel,
        out_shape=jax.ShapeDtypeStruct(shape, backs[0].dtype),
        in_specs=[pl.BlockSpec(memory_space=pltpu.VMEM)] * 4,
        out_specs=pl.BlockSpec(memory_space=pl.ANY),
        scratch_shapes=[pltpu.VMEM(shape, backs[0].dtype), pltpu.SemaphoreType.DMA((6,))],
        compiler_params=pltpu.CompilerParams(vmem_limit_bytes=LIMIT),
    )(*backs)


def body(factors, occ_energy, vir_energy, shifts):
    count_x, count_z = lax.axis_size("kxy"), lax.axis_size("kz")
    odd, after, before = routes(count_x, count_z)
    route_a = {**onto(odd, 0), **onto(after, 1)}
    route_b = {**onto(odd, 1), **onto(before, 0)}
    route_after = onto(after, 1)
    route_before = onto(before, 0)
    cores = {i: i ^ count_z for i in range(count_x * count_z)}
    route_early = {t: s for s, t in route_after.items()} | {t: s ^ count_z for s, t in route_before.items()}
    downward = {s: t for s, t in cores.items() if s > t}
    upward = {s: t for s, t in cores.items() if s < t}

    own = factors[0, 0]
    arrived_a = move(own, route_a)
    arrived_b = move(own, route_before)

    occ_a = move(occ_energy[0], route_a)
    occ_b = move(occ_energy[0], route_b)

    def send_energies(by_x, by_z):
        def send(vir):
            return tuple(
                move(vir, moved_from(route, by_x, by_z, count_x, count_z)) for route in (route_a, route_b)
            )

        return send

    span = REACH - 1
    sends = [send_energies(1 + i // span, 1 + i % span) for i in range(span * span)]
    vir_a, vir_b = lax.switch((shifts[0, 0] - 1) * span + shifts[0, 1] - 1, sends, vir_energy[0])
    arrived_a, vir_a, vir_b = lax.optimization_barrier((arrived_a, vir_a, vir_b))
    crossed = move(arrived_a, upward)
    w = choose(arrived_b, arrived_a, False)
    gap_o, gap_w = gaps(vir_a, vir_b, occ_a, occ_b)
    o = choose(arrived_a, crossed, True)

    to_a, to_f = block(o[0], w[0], gap_o[0], gap_w[0])
    to_b, to_f = block(o[1], w[0], gap_o[1], gap_w[0], old_w=to_f)
    back_early = move(to_f, route_early)
    to_b, to_s = block(o[1], w[1], gap_o[1], gap_w[1], old_o=to_b)
    met = move(to_b, cores)
    to_a, to_s = block(o[0], w[1], gap_o[0], gap_w[1], to_a, to_s)
    for_a, for_b = merge(to_a, met, to_s)
    back_a = move_back(for_a, route_a)
    back_b = move_back(for_b, route_b)
    lowered = move(back_early, downward)
    return finish(back_early, lowered, back_a, back_b)[None, None]


def solution(mesh):
    placed = (P("kxy", "kz", None, None, None), P("kxy", "kz", None), P("kxy", "kz", None), P())
    return jax.shard_map(
        body,
        mesh=mesh,
        in_specs=placed,
        out_specs=P("kxy", "kz", None, None, None),
        check_vma=False,
    )
```

```python
import functools

import jax
import jax.numpy as jnp
from jax import lax
from jax.experimental import pallas as pl
from jax.experimental.pallas import tpu as pltpu
from jax.sharding import PartitionSpec as P


REACH = 4
LIMIT = 24 << 20
AXES = ("kxy", "kz")
MEET_Z = ((0, 0, 1, 1), (3, 2, 3, 3), (3, 2, 3, 3), (1, 0, 0, 0))
AROUND_AFTER = {(1, 3): (1, 3, 1), (3, 1): (3, 1, 1), (3, 2): (3, 2, 1), (3, 3): (3, 3, 1)}
AROUND_BEFORE = {(0, 0): (0, 0, 0), (0, 1): (0, 1, 0), (0, 2): (0, 2, 0), (0, 3): (0, 3, 0)}
PARTED_AFTER = {(3, 0): (3, 3, 0)}
PARTED_BEFORE = {(1, 1): (0, 1, 1)}


def coordinates(kx, kz):
    return kz % 4, (kx // 2) % 4, 2 * (kz // 4) + kx // 8


def device(x, y, z, core):
    return (8 * (z % 2) + 2 * (y % 4) + core) * 8 + 4 * (z // 2) + x


def routes(count_x, count_z):
    odd, after, before = {}, {}, {}
    for kx in range(1, count_x, 2):
        for kz in range(count_z):
            x, y, z = coordinates(kx, kz)
            meet = (x, y - 1, z ^ MEET_Z[x][y])
            odd[kx * count_z + kz] = meet
            after[(kx + 3) % count_x * count_z + (kz + 3) % count_z] = meet
            before[(kx - 3) % count_x * count_z + (kz - 3) % count_z] = meet
    return odd, after, before


def around(meets, core, table, count_z):
    first, second, homes = {}, {}, set()
    for home, (x, y, z) in meets.items():
        if (x, y % 4) in table:
            column_x, column_y, column_core = table[x, y % 4]
            middle = device(column_x, column_y, coordinates(*divmod(home, count_z))[2], column_core)
            first[device(x, y, z, core)] = middle
            second[middle] = home
            homes.add(home)
    return first, second, homes


def onto(meets, core):
    return {source: device(*meet, core) for source, meet in meets.items()}


def move(x, route):
    return lax.ppermute(x, AXES, sorted(route.items()))


def move_back(x, route):
    return lax.ppermute(x, AXES, sorted((t, s) for s, t in route.items()))


def split(x):
    high = x.astype(jnp.bfloat16)
    return high, (x - high.astype(jnp.float32)).astype(jnp.bfloat16)


def left(x, axis):
    high, low = split(x)
    return jnp.concatenate([high, high, low], axis)


def right(x, axis):
    high, low = split(x)
    return jnp.concatenate([high, low, high], axis)


def product(x, y, inner_x, inner_y):
    return lax.dot_general(
        x, y, (((inner_x,), (inner_y,)), ((), ())), preferred_element_type=jnp.float32
    )


def on_upper():
    return lax.axis_index("kxy") % 2 == 1


def block_kernel(has_o, has_w, *refs):
    o_ref, w_ref, gap_o, gap_w, *refs = refs
    old_o = refs.pop(0) if has_o else None
    old_w = refs.pop(0) if has_w else None
    to_o, to_w, tall, flat = refs
    inner = to_o.shape[1]

    a, b = o_ref[0], o_ref[1]
    for i, x in enumerate((a, b, a + b)):
        flat[i] = left(x, 1)
        high, low = split(x.T)
        tall[i, :, :inner] = high
        tall[i, :, inner : 2 * inner] = high
        tall[i, :, 2 * inner :] = low
    c, d = w_ref[0], w_ref[1]
    ac = product(tall[0], right(c, 0), 1, 0)
    bd = product(tall[1], right(d, 0), 1, 0)
    both = product(tall[2], right(c - d, 0), 1, 0)
    inverse = 1.0 / (gap_o[...] + gap_w[...])
    p = (ac + bd) * inverse
    q = (both - ac + bd) * inverse
    cp = product(left(c, 1), right(p, 1), 1, 1)
    dq = product(left(d, 1), right(q, 1), 1, 1)
    both = product(left(c + d, 1), right(p + q, 1), 1, 1)
    re, im = cp - dq, both - cp - dq
    to_o[0] = re + old_o[0] if has_o else re
    to_o[1] = im + old_o[1] if has_o else im
    ap = product(flat[0], right(p, 0), 1, 0)
    bq = product(flat[1], right(q, 0), 1, 0)
    both = product(flat[2], right(p - q, 0), 1, 0)
    re, im = ap + bq, both - ap + bq
    to_w[0] = re + old_w[0] if has_w else re
    to_w[1] = im + old_w[1] if has_w else im


def block(o, w, gap_o, gap_w, old_o=None, old_w=None):
    parts, inner, half = o.shape
    old = [x for x in (old_o, old_w) if x is not None]
    spec = pl.BlockSpec(memory_space=pltpu.VMEM)
    return pl.pallas_call(
        functools.partial(block_kernel, old_o is not None, old_w is not None),
        out_shape=(jax.ShapeDtypeStruct((parts, inner, half), jnp.float32),) * 2,
        in_specs=[spec] * (4 + len(old)),
        out_specs=(spec, spec),
        scratch_shapes=[
            pltpu.VMEM((3, half, 3 * inner), jnp.bfloat16),
            pltpu.VMEM((3, inner, 3 * half), jnp.bfloat16),
        ],
        compiler_params=pltpu.CompilerParams(vmem_limit_bytes=LIMIT),
        cost_estimate=pl.CostEstimate(
            flops=54 * inner * half * half, bytes_accessed=32 * inner * half, transcendentals=half * half
        ),
    )(o, w, gap_o, gap_w, *old)


def moved_from(route, by_x, by_z, count_x, count_z):
    out = {}
    for k, target in route.items():
        kx, kz = divmod(k, count_z)
        out[(kx + by_x) % count_x * count_z + (kz + by_z) % count_z] = target
    return out


def choose_kernel(turned, if_lower, if_upper, first, second, sems):
    half = first.shape[2]
    upper = on_upper()

    def copies(source, turned):
        at = [pl.ds(i * half, half) for i in ((1, 0) if turned else (0, 1))]
        return (
            pltpu.make_async_copy(source.at[:, :, at[0]], first, sems.at[0]),
            pltpu.make_async_copy(source.at[:, :, at[1]], second, sems.at[1]),
        )

    @pl.when(upper)
    def _():
        for copy in copies(if_upper, turned):
            copy.start()

    @pl.when(jnp.logical_not(upper))
    def _():
        for copy in copies(if_lower, False):
            copy.start()

    for copy in copies(if_lower, False):
        copy.wait()


def choose(if_lower, if_upper, turned):
    parts, inner, pairs = if_lower.shape
    spec = pl.BlockSpec(memory_space=pltpu.VMEM)
    return pl.pallas_call(
        functools.partial(choose_kernel, turned),
        out_shape=(jax.ShapeDtypeStruct((parts, inner, pairs // 2), if_lower.dtype),) * 2,
        in_specs=[pl.BlockSpec(memory_space=pl.ANY)] * 2,
        out_specs=(spec, spec),
        scratch_shapes=[pltpu.SemaphoreType.DMA((2,))],
        compiler_params=pltpu.CompilerParams(vmem_limit_bytes=LIMIT),
        cost_estimate=pl.CostEstimate(flops=0, bytes_accessed=8 * if_lower.size, transcendentals=0),
    )(if_lower, if_upper)


def gap_kernel(vir_a, vir_b, occ_a, occ_b, first_o, second_o, first_w, second_w):
    upper = on_upper()
    occ_o = jnp.where(upper, occ_b[...], occ_a[...])
    occ_w = jnp.where(upper, occ_a[...], occ_b[...])
    vir_o = jnp.where(upper, vir_b[...], vir_a[...])
    vir_w = jnp.where(upper, vir_a[...], vir_b[...])
    span = vir_o.shape[1]
    vir_o = jnp.broadcast_to(vir_o, (8, span)).T[:, :1]
    each = first_o.shape[0] // span
    for i in range(each):
        lower_occ, upper_occ = occ_o[:, i : i + 1], occ_o[:, each + i : each + i + 1]
        at = pl.ds(i * span, span)
        first_o[at, :] = vir_o - jnp.where(upper, upper_occ, lower_occ)
        second_o[at, :] = vir_o - jnp.where(upper, lower_occ, upper_occ)
        first_w[:, at] = vir_w - occ_w[:, i : i + 1]
        second_w[:, at] = vir_w - occ_w[:, each + i : each + i + 1]


def gaps(vir_a, vir_b, occ_a, occ_b):
    half = vir_a.shape[1] * occ_a.shape[1] // 2
    spec = pl.BlockSpec(memory_space=pltpu.VMEM)
    column = jax.ShapeDtypeStruct((half, 1), vir_a.dtype)
    row = jax.ShapeDtypeStruct((1, half), vir_a.dtype)
    out = pl.pallas_call(
        gap_kernel,
        out_shape=(column, column, row, row),
        in_specs=[spec] * 4,
        out_specs=(spec,) * 4,
        compiler_params=pltpu.CompilerParams(vmem_limit_bytes=LIMIT),
    )(vir_a, vir_b, occ_a, occ_b)
    return out[:2], out[2:]


def merge_kernel(to_a, met, to_s, for_a, for_b, for_re, for_im):
    own = to_a[...] + met[...]
    other = to_s[...]
    upper = on_upper()
    for_a[...] = jnp.where(upper, other, own)
    for_b[...] = jnp.where(upper, own, other)
    for_re[...] = other[0]
    for_im[...] = other[1]


def merge(to_a, met, to_s):
    spec = pl.BlockSpec(memory_space=pltpu.VMEM)
    whole = jax.ShapeDtypeStruct(to_a.shape, to_a.dtype)
    part = jax.ShapeDtypeStruct(to_a.shape[1:], to_a.dtype)
    return pl.pallas_call(
        merge_kernel,
        out_shape=(whole, whole, part, part),
        in_specs=[spec] * 3,
        out_specs=(spec,) * 4,
        compiler_params=pltpu.CompilerParams(vmem_limit_bytes=LIMIT),
    )(to_a, met, to_s)


def finish_kernel(early, lowered, back_a, back_b, hop, back_re, back_im, out, held, sems):
    half = back_a.shape[2]
    steps = sems.shape[0]
    rows = back_a.shape[1] // steps
    upper = on_upper()
    copies = []
    for i in range(steps):
        at = pl.ds(i * rows, rows)
        a, b = back_a[:, at], back_b[:, at]
        held[:, at, :half] = -jnp.where(upper, a, early[:, at] + lowered[:, at])
        even = a + b + hop[:, at]
        held[0, at, half:] = -jnp.where(upper, b[0], even[0] + back_re[at])
        held[1, at, half:] = -jnp.where(upper, b[1], even[1] + back_im[at])
        copies.append(pltpu.make_async_copy(held.at[:, at], out.at[:, at], sems.at[i]))
        copies[-1].start()
    for copy in copies:
        copy.wait()


def finish(*backs):
    parts, inner, half = backs[0].shape
    shape = (parts, inner, 2 * half)
    return pl.pallas_call(
        finish_kernel,
        out_shape=jax.ShapeDtypeStruct(shape, backs[0].dtype),
        in_specs=[pl.BlockSpec(memory_space=pltpu.VMEM)] * 7,
        out_specs=pl.BlockSpec(memory_space=pl.ANY),
        scratch_shapes=[pltpu.VMEM(shape, backs[0].dtype), pltpu.SemaphoreType.DMA((6,))],
        compiler_params=pltpu.CompilerParams(vmem_limit_bytes=LIMIT),
    )(*backs)


def body(factors, occ_energy, vir_energy, shifts):
    count_x, count_z = lax.axis_size("kxy"), lax.axis_size("kz")
    odd, after, before = routes(count_x, count_z)
    route_a = {**onto(odd, 0), **onto(after, 1)}
    route_b = {**onto(odd, 1), **onto(before, 0)}
    route_after = onto(after, 1)
    route_before = onto(before, 0)
    cores = {i: i ^ count_z for i in range(count_x * count_z)}
    route_early = {t: s for s, t in route_after.items()} | {t: s ^ count_z for s, t in route_before.items()}
    first_after, second_after, homes_after = around(after, 1, AROUND_AFTER, count_z)
    first_before, second_before, homes_before = around(before, 0, AROUND_BEFORE, count_z)
    first_hop = {**first_after, **first_before}
    second_hop = {**second_after, **second_before}
    part_after, leave_after, parted_after = around(after, 1, PARTED_AFTER, count_z)
    part_before, leave_before, parted_before = around(before, 0, PARTED_BEFORE, count_z)
    part_hop = {**part_after, **part_before}
    leave_hop = {**leave_after, **leave_before}
    straight = {route_after[s]: s for s in parted_after} | {route_before[s]: s for s in parted_before}
    not_a, not_b = homes_after | parted_after, homes_before | parted_before
    late_a = {**onto(odd, 0), **{s: t for s, t in route_after.items() if s not in not_a}}
    late_b = {**onto(odd, 1), **{s: t for s, t in route_before.items() if s not in not_b}}
    downward = {s: t for s, t in cores.items() if s > t}
    upward = {s: t for s, t in cores.items() if s < t}

    own = factors[0, 0]
    arrived_a = move(own, route_a)
    arrived_b = move(own, route_before)

    occ_a = move(occ_energy[0], route_a)
    occ_b = move(occ_energy[0], route_b)

    def send_energies(by_x, by_z):
        def send(vir):
            return tuple(
                move(vir, moved_from(route, by_x, by_z, count_x, count_z)) for route in (route_a, route_b)
            )

        return send

    span = REACH - 1
    sends = [send_energies(1 + i // span, 1 + i % span) for i in range(span * span)]
    vir_a, vir_b = lax.switch((shifts[0, 0] - 1) * span + shifts[0, 1] - 1, sends, vir_energy[0])
    arrived_a, vir_a, vir_b = lax.optimization_barrier((arrived_a, vir_a, vir_b))
    crossed = move(arrived_a, upward)
    w = choose(arrived_b, arrived_a, False)
    gap_o, gap_w = gaps(vir_a, vir_b, occ_a, occ_b)
    o = choose(arrived_a, crossed, True)

    to_a, to_f = block(o[0], w[0], gap_o[0], gap_w[0])
    to_b, to_f = block(o[1], w[0], gap_o[1], gap_w[0], old_w=to_f)
    back_early = move(to_f, route_early)
    to_b, to_s = block(o[1], w[1], gap_o[1], gap_w[1], old_o=to_b)
    met = move(to_b, cores)
    to_a, to_s = block(o[0], w[1], gap_o[0], gap_w[1], to_a, to_s)
    middle = move(to_s, first_hop)
    for_a, for_b, for_re, for_im = merge(to_a, met, to_s)
    part = move(for_im, part_hop)
    back_a = move_back(for_a, late_a)
    back_b = move_back(for_b, late_b)
    back_re = move(for_re, straight)
    lowered = move(back_early, downward)
    hop = move(middle, second_hop)
    back_im = move(part, leave_hop)
    return finish(back_early, lowered, back_a, back_b, hop, back_re, back_im)[None, None]


def solution(mesh):
    placed = (P("kxy", "kz", None, None, None), P("kxy", "kz", None), P("kxy", "kz", None), P())
    return jax.shard_map(
        body,
        mesh=mesh,
        in_specs=placed,
        out_specs=P("kxy", "kz", None, None, None),
        check_vma=False,
    )
```

```python
import functools

import jax
import jax.numpy as jnp
from jax import lax
from jax.experimental import pallas as pl
from jax.experimental.pallas import tpu as pltpu
from jax.sharding import PartitionSpec as P


REACH = 4
LIMIT = 24 << 20
AXES = ("kxy", "kz")
MEET_Z = ((0, 0, 1, 1), (3, 2, 3, 3), (3, 2, 3, 3), (1, 0, 0, 0))
AROUND_AFTER = {(1, 3): (1, 3, 1), (3, 1): (3, 1, 1), (3, 2): (3, 2, 1), (3, 3): (3, 3, 1)}
AROUND_BEFORE = {(0, 0): (0, 0, 0), (0, 1): (0, 1, 0), (0, 2): (0, 2, 0), (0, 3): (0, 3, 0)}
PARTED_AFTER = {(3, 0): (3, 3, 0)}
PARTED_BEFORE = {(1, 1): (0, 1, 1)}


def coordinates(kx, kz):
    return kz % 4, (kx // 2) % 4, 2 * (kz // 4) + kx // 8


def device(x, y, z, core):
    return (8 * (z % 2) + 2 * (y % 4) + core) * 8 + 4 * (z // 2) + x


def routes(count_x, count_z):
    odd, after, before = {}, {}, {}
    for kx in range(1, count_x, 2):
        for kz in range(count_z):
            x, y, z = coordinates(kx, kz)
            meet = (x, y - 1, z ^ MEET_Z[x][y])
            odd[kx * count_z + kz] = meet
            after[(kx + 3) % count_x * count_z + (kz + 3) % count_z] = meet
            before[(kx - 3) % count_x * count_z + (kz - 3) % count_z] = meet
    return odd, after, before


def around(meets, core, table, count_z):
    first, second, homes = {}, {}, set()
    for home, (x, y, z) in meets.items():
        if (x, y % 4) in table:
            column_x, column_y, column_core = table[x, y % 4]
            middle = device(column_x, column_y, coordinates(*divmod(home, count_z))[2], column_core)
            first[device(x, y, z, core)] = middle
            second[middle] = home
            homes.add(home)
    return first, second, homes


def onto(meets, core):
    return {source: device(*meet, core) for source, meet in meets.items()}


def move(x, route):
    return lax.ppermute(x, AXES, sorted(route.items()))


def move_back(x, route):
    return lax.ppermute(x, AXES, sorted((t, s) for s, t in route.items()))


def split(x):
    high = x.astype(jnp.bfloat16)
    return high, (x - high.astype(jnp.float32)).astype(jnp.bfloat16)


def left(x, axis):
    high, low = split(x)
    return jnp.concatenate([high, high, low], axis)


def right(x, axis):
    high, low = split(x)
    return jnp.concatenate([high, low, high], axis)


def product(x, y, inner_x, inner_y):
    return lax.dot_general(
        x, y, (((inner_x,), (inner_y,)), ((), ())), preferred_element_type=jnp.float32
    )


def on_upper():
    return lax.axis_index("kxy") % 2 == 1


def block_kernel(has_o, has_w, parted, *refs):
    o_ref, w_ref, gap_o, gap_w, *refs = refs
    old_o = refs.pop(0) if has_o else None
    old_w = refs.pop(0) if has_w else None
    to_o, *to_w, tall, flat = refs
    inner = to_o.shape[1]

    a, b = o_ref[0], o_ref[1]
    for i, x in enumerate((a, b, a + b)):
        flat[i] = left(x, 1)
        high, low = split(x.T)
        tall[i, :, :inner] = high
        tall[i, :, inner : 2 * inner] = high
        tall[i, :, 2 * inner :] = low
    c, d = w_ref[0], w_ref[1]
    ac = product(tall[0], right(c, 0), 1, 0)
    bd = product(tall[1], right(d, 0), 1, 0)
    both = product(tall[2], right(c - d, 0), 1, 0)
    inverse = 1.0 / (gap_o[...] + gap_w[...])
    p = (ac + bd) * inverse
    q = (both - ac + bd) * inverse
    cp = product(left(c, 1), right(p, 1), 1, 1)
    dq = product(left(d, 1), right(q, 1), 1, 1)
    both = product(left(c + d, 1), right(p + q, 1), 1, 1)
    re, im = cp - dq, both - cp - dq
    to_o[0] = re + old_o[0] if has_o else re
    to_o[1] = im + old_o[1] if has_o else im
    ap = product(flat[0], right(p, 0), 1, 0)
    bq = product(flat[1], right(q, 0), 1, 0)
    both = product(flat[2], right(p - q, 0), 1, 0)
    re, im = ap + bq, both - ap + bq
    re = re + old_w[0] if has_w else re
    im = im + old_w[1] if has_w else im
    if parted:
        to_w[0][...] = re
        to_w[1][...] = im
    else:
        to_w[0][0] = re
        to_w[0][1] = im


def block(o, w, gap_o, gap_w, old_o=None, old_w=None, parted=False):
    parts, inner, half = o.shape
    old = [x for x in (old_o, old_w) if x is not None]
    whole = jax.ShapeDtypeStruct((parts, inner, half), jnp.float32)
    part = jax.ShapeDtypeStruct((inner, half), jnp.float32)
    out_shape = (whole, part, part) if parted else (whole, whole)
    spec = pl.BlockSpec(memory_space=pltpu.VMEM)
    return pl.pallas_call(
        functools.partial(block_kernel, old_o is not None, old_w is not None, parted),
        out_shape=out_shape,
        in_specs=[spec] * (4 + len(old)),
        out_specs=(spec,) * len(out_shape),
        scratch_shapes=[
            pltpu.VMEM((3, half, 3 * inner), jnp.bfloat16),
            pltpu.VMEM((3, inner, 3 * half), jnp.bfloat16),
        ],
        compiler_params=pltpu.CompilerParams(vmem_limit_bytes=LIMIT),
        cost_estimate=pl.CostEstimate(
            flops=54 * inner * half * half, bytes_accessed=32 * inner * half, transcendentals=half * half
        ),
    )(o, w, gap_o, gap_w, *old)


def moved_from(route, by_x, by_z, count_x, count_z):
    out = {}
    for k, target in route.items():
        kx, kz = divmod(k, count_z)
        out[(kx + by_x) % count_x * count_z + (kz + by_z) % count_z] = target
    return out


def choose_kernel(turned, if_lower, if_upper, first, second, sems):
    half = first.shape[2]
    upper = on_upper()

    def copies(source, turned):
        at = [pl.ds(i * half, half) for i in ((1, 0) if turned else (0, 1))]
        return (
            pltpu.make_async_copy(source.at[:, :, at[0]], first, sems.at[0]),
            pltpu.make_async_copy(source.at[:, :, at[1]], second, sems.at[1]),
        )

    @pl.when(upper)
    def _():
        for copy in copies(if_upper, turned):
            copy.start()

    @pl.when(jnp.logical_not(upper))
    def _():
        for copy in copies(if_lower, False):
            copy.start()

    for copy in copies(if_lower, False):
        copy.wait()


def choose(if_lower, if_upper, turned):
    parts, inner, pairs = if_lower.shape
    spec = pl.BlockSpec(memory_space=pltpu.VMEM)
    return pl.pallas_call(
        functools.partial(choose_kernel, turned),
        out_shape=(jax.ShapeDtypeStruct((parts, inner, pairs // 2), if_lower.dtype),) * 2,
        in_specs=[pl.BlockSpec(memory_space=pl.ANY)] * 2,
        out_specs=(spec, spec),
        scratch_shapes=[pltpu.SemaphoreType.DMA((2,))],
        compiler_params=pltpu.CompilerParams(vmem_limit_bytes=LIMIT),
        cost_estimate=pl.CostEstimate(flops=0, bytes_accessed=8 * if_lower.size, transcendentals=0),
    )(if_lower, if_upper)


def gap_kernel(vir_a, vir_b, occ_a, occ_b, first_o, second_o, first_w, second_w):
    upper = on_upper()
    occ_o = jnp.where(upper, occ_b[...], occ_a[...])
    occ_w = jnp.where(upper, occ_a[...], occ_b[...])
    vir_o = jnp.where(upper, vir_b[...], vir_a[...])
    vir_w = jnp.where(upper, vir_a[...], vir_b[...])
    span = vir_o.shape[1]
    vir_o = jnp.broadcast_to(vir_o, (8, span)).T[:, :1]
    each = first_o.shape[0] // span
    for i in range(each):
        lower_occ, upper_occ = occ_o[:, i : i + 1], occ_o[:, each + i : each + i + 1]
        at = pl.ds(i * span, span)
        first_o[at, :] = vir_o - jnp.where(upper, upper_occ, lower_occ)
        second_o[at, :] = vir_o - jnp.where(upper, lower_occ, upper_occ)
        first_w[:, at] = vir_w - occ_w[:, i : i + 1]
        second_w[:, at] = vir_w - occ_w[:, each + i : each + i + 1]


def gaps(vir_a, vir_b, occ_a, occ_b):
    half = vir_a.shape[1] * occ_a.shape[1] // 2
    spec = pl.BlockSpec(memory_space=pltpu.VMEM)
    column = jax.ShapeDtypeStruct((half, 1), vir_a.dtype)
    row = jax.ShapeDtypeStruct((1, half), vir_a.dtype)
    out = pl.pallas_call(
        gap_kernel,
        out_shape=(column, column, row, row),
        in_specs=[spec] * 4,
        out_specs=(spec,) * 4,
        compiler_params=pltpu.CompilerParams(vmem_limit_bytes=LIMIT),
    )(vir_a, vir_b, occ_a, occ_b)
    return out[:2], out[2:]


def merge_kernel(to_a, met, re, im, for_a, for_b):
    upper = on_upper()
    for i, other in enumerate((re[...], im[...])):
        own = to_a[i] + met[i]
        for_a[i] = jnp.where(upper, other, own)
        for_b[i] = jnp.where(upper, own, other)


def merge(to_a, met, re, im):
    spec = pl.BlockSpec(memory_space=pltpu.VMEM)
    return pl.pallas_call(
        merge_kernel,
        out_shape=(jax.ShapeDtypeStruct(to_a.shape, to_a.dtype),) * 2,
        in_specs=[spec] * 4,
        out_specs=(spec, spec),
        compiler_params=pltpu.CompilerParams(vmem_limit_bytes=LIMIT),
    )(to_a, met, re, im)


def finish_kernel(early, lowered, back_a, back_b, hop_re, hop_im, back_re, back_im, out, held, sems):
    half = back_a.shape[2]
    steps = sems.shape[0]
    rows = back_a.shape[1] // steps
    upper = on_upper()
    copies = []
    for i in range(steps):
        at = pl.ds(i * rows, rows)
        a, b = back_a[:, at], back_b[:, at]
        held[:, at, :half] = -jnp.where(upper, a, early[:, at] + lowered[:, at])
        even = a + b
        held[0, at, half:] = -jnp.where(upper, b[0], even[0] + hop_re[at] + back_re[at])
        held[1, at, half:] = -jnp.where(upper, b[1], even[1] + hop_im[at] + back_im[at])
        copies.append(pltpu.make_async_copy(held.at[:, at], out.at[:, at], sems.at[i]))
        copies[-1].start()
    for copy in copies:
        copy.wait()


def finish(*backs):
    parts, inner, half = backs[0].shape
    shape = (parts, inner, 2 * half)
    return pl.pallas_call(
        finish_kernel,
        out_shape=jax.ShapeDtypeStruct(shape, backs[0].dtype),
        in_specs=[pl.BlockSpec(memory_space=pltpu.VMEM)] * 8,
        out_specs=pl.BlockSpec(memory_space=pl.ANY),
        scratch_shapes=[pltpu.VMEM(shape, backs[0].dtype), pltpu.SemaphoreType.DMA((6,))],
        compiler_params=pltpu.CompilerParams(vmem_limit_bytes=LIMIT),
    )(*backs)


def body(factors, occ_energy, vir_energy, shifts):
    count_x, count_z = lax.axis_size("kxy"), lax.axis_size("kz")
    odd, after, before = routes(count_x, count_z)
    route_a = {**onto(odd, 0), **onto(after, 1)}
    route_b = {**onto(odd, 1), **onto(before, 0)}
    route_after = onto(after, 1)
    route_before = onto(before, 0)
    cores = {i: i ^ count_z for i in range(count_x * count_z)}
    route_early = {t: s for s, t in route_after.items()} | {t: s ^ count_z for s, t in route_before.items()}
    first_after, second_after, homes_after = around(after, 1, AROUND_AFTER, count_z)
    first_before, second_before, homes_before = around(before, 0, AROUND_BEFORE, count_z)
    first_hop = {**first_after, **first_before}
    second_hop = {**second_after, **second_before}
    part_after, leave_after, parted_after = around(after, 1, PARTED_AFTER, count_z)
    part_before, leave_before, parted_before = around(before, 0, PARTED_BEFORE, count_z)
    part_hop = {**part_after, **part_before}
    leave_hop = {**leave_after, **leave_before}
    straight = {route_after[s]: s for s in parted_after} | {route_before[s]: s for s in parted_before}
    not_a, not_b = homes_after | parted_after, homes_before | parted_before
    late_a = {**onto(odd, 0), **{s: t for s, t in route_after.items() if s not in not_a}}
    late_b = {**onto(odd, 1), **{s: t for s, t in route_before.items() if s not in not_b}}
    downward = {s: t for s, t in cores.items() if s > t}
    upward = {s: t for s, t in cores.items() if s < t}

    own = factors[0, 0]
    arrived_a = move(own, route_a)
    arrived_b = move(own, route_before)

    occ_a = move(occ_energy[0], route_a)
    occ_b = move(occ_energy[0], route_b)

    def send_energies(by_x, by_z):
        def send(vir):
            return tuple(
                move(vir, moved_from(route, by_x, by_z, count_x, count_z)) for route in (route_a, route_b)
            )

        return send

    span = REACH - 1
    sends = [send_energies(1 + i // span, 1 + i % span) for i in range(span * span)]
    vir_a, vir_b = lax.switch((shifts[0, 0] - 1) * span + shifts[0, 1] - 1, sends, vir_energy[0])
    arrived_a, vir_a, vir_b = lax.optimization_barrier((arrived_a, vir_a, vir_b))
    crossed = move(arrived_a, upward)
    w = choose(arrived_b, arrived_a, False)
    gap_o, gap_w = gaps(vir_a, vir_b, occ_a, occ_b)
    o = choose(arrived_a, crossed, True)

    to_a, to_f = block(o[0], w[0], gap_o[0], gap_w[0])
    to_b, to_f = block(o[1], w[0], gap_o[1], gap_w[0], old_w=to_f)
    back_early = move(to_f, route_early)
    to_b, to_s = block(o[1], w[1], gap_o[1], gap_w[1], old_o=to_b)
    met = move(to_b, cores)
    to_a, re, im = block(o[0], w[1], gap_o[0], gap_w[1], to_a, to_s, parted=True)
    middle_re = move(re, first_hop)
    middle_im = move(im, first_hop | part_hop)
    for_a, for_b = merge(to_a, met, re, im)
    back_a = move_back(for_a, late_a)
    back_b = move_back(for_b, late_b)
    back_re = move(re, straight)
    hop_re = move(middle_re, second_hop)
    hop_im = move(middle_im, second_hop)
    back_im = move(middle_im, leave_hop)
    lowered = move(back_early, downward)
    return finish(back_early, lowered, back_a, back_b, hop_re, hop_im, back_re, back_im)[None, None]


def solution(mesh):
    placed = (P("kxy", "kz", None, None, None), P("kxy", "kz", None), P("kxy", "kz", None), P())
    return jax.shard_map(
        body,
        mesh=mesh,
        in_specs=placed,
        out_specs=P("kxy", "kz", None, None, None),
        check_vma=False,
    )
```

```python
import functools

import jax
import jax.numpy as jnp
from jax import lax
from jax.experimental import pallas as pl
from jax.experimental.pallas import tpu as pltpu
from jax.sharding import PartitionSpec as P


REACH = 4
LIMIT = 24 << 20
AXES = ("kxy", "kz")
MEET_Z = ((0, 0, 1, 1), (3, 2, 3, 3), (3, 2, 3, 3), (1, 0, 0, 0))
AROUND_AFTER = {(1, 3): (1, 3, 1), (3, 1): (3, 1, 1), (3, 2): (3, 2, 1), (3, 3): (3, 3, 1)}
AROUND_BEFORE = {(0, 0): (0, 0, 0), (0, 1): (0, 1, 0), (0, 2): (0, 2, 0), (0, 3): (0, 3, 0)}
PARTED_AFTER = {(3, 0): (3, 3, 0)}
PARTED_BEFORE = {(1, 1): (0, 1, 1)}


def coordinates(kx, kz):
    return kz % 4, (kx // 2) % 4, 2 * (kz // 4) + kx // 8


def device(x, y, z, core):
    return (8 * (z % 2) + 2 * (y % 4) + core) * 8 + 4 * (z // 2) + x


def routes(count_x, count_z):
    odd, after, before = {}, {}, {}
    for kx in range(1, count_x, 2):
        for kz in range(count_z):
            x, y, z = coordinates(kx, kz)
            meet = (x, y - 1, z ^ MEET_Z[x][y])
            odd[kx * count_z + kz] = meet
            after[(kx + 3) % count_x * count_z + (kz + 3) % count_z] = meet
            before[(kx - 3) % count_x * count_z + (kz - 3) % count_z] = meet
    return odd, after, before


def around(meets, core, table, count_z):
    first, second, homes = {}, {}, set()
    for home, (x, y, z) in meets.items():
        if (x, y % 4) in table:
            column_x, column_y, column_core = table[x, y % 4]
            middle = device(column_x, column_y, coordinates(*divmod(home, count_z))[2], column_core)
            first[device(x, y, z, core)] = middle
            second[middle] = home
            homes.add(home)
    return first, second, homes


def onto(meets, core):
    return {source: device(*meet, core) for source, meet in meets.items()}


def move(x, route):
    return lax.ppermute(x, AXES, sorted(route.items()))


def move_back(x, route):
    return lax.ppermute(x, AXES, sorted((t, s) for s, t in route.items()))


def split(x):
    high = x.astype(jnp.bfloat16)
    return high, (x - high.astype(jnp.float32)).astype(jnp.bfloat16)


def left(x, axis):
    high, low = split(x)
    return jnp.concatenate([high, high, low], axis)


def right(x, axis):
    high, low = split(x)
    return jnp.concatenate([high, low, high], axis)


def product(x, y, inner_x, inner_y):
    return lax.dot_general(
        x, y, (((inner_x,), (inner_y,)), ((), ())), preferred_element_type=jnp.float32
    )


def on_upper():
    return lax.axis_index("kxy") % 2 == 1


def block_kernel(has_o, has_w, parted, *refs):
    o_ref, w_ref, gap_o, gap_w, *refs = refs
    old_o = refs.pop(0) if has_o else None
    old_w = refs.pop(0) if has_w else None
    to_o, *to_w, tall, flat = refs
    inner = to_o.shape[1]

    a, b = o_ref[0], o_ref[1]
    for i, x in enumerate((a, b, a + b)):
        flat[i] = left(x, 1)
        high, low = split(x.T)
        tall[i, :, :inner] = high
        tall[i, :, inner : 2 * inner] = high
        tall[i, :, 2 * inner :] = low
    c, d = w_ref[0], w_ref[1]
    ac = product(tall[0], right(c, 0), 1, 0)
    bd = product(tall[1], right(d, 0), 1, 0)
    both = product(tall[2], right(c - d, 0), 1, 0)
    inverse = 1.0 / (gap_o[...] + gap_w[...])
    p = (ac + bd) * inverse
    q = (both - ac + bd) * inverse
    cp = product(left(c, 1), right(p, 1), 1, 1)
    dq = product(left(d, 1), right(q, 1), 1, 1)
    both = product(left(c + d, 1), right(p + q, 1), 1, 1)
    re, im = cp - dq, both - cp - dq
    to_o[0] = re + old_o[0] if has_o else re
    to_o[1] = im + old_o[1] if has_o else im
    ap = product(flat[0], right(p, 0), 1, 0)
    bq = product(flat[1], right(q, 0), 1, 0)
    both = product(flat[2], right(p - q, 0), 1, 0)
    re, im = ap + bq, both - ap + bq
    re = re + old_w[0] if has_w else re
    im = im + old_w[1] if has_w else im
    if parted:
        to_w[0][...] = re
        to_w[1][...] = im
    else:
        to_w[0][0] = re
        to_w[0][1] = im


def block(o, w, gap_o, gap_w, old_o=None, old_w=None, parted=False):
    parts, inner, half = o.shape
    old = [x for x in (old_o, old_w) if x is not None]
    whole = jax.ShapeDtypeStruct((parts, inner, half), jnp.float32)
    part = jax.ShapeDtypeStruct((inner, half), jnp.float32)
    out_shape = (whole, part, part) if parted else (whole, whole)
    spec = pl.BlockSpec(memory_space=pltpu.VMEM)
    return pl.pallas_call(
        functools.partial(block_kernel, old_o is not None, old_w is not None, parted),
        out_shape=out_shape,
        in_specs=[spec] * (4 + len(old)),
        out_specs=(spec,) * len(out_shape),
        scratch_shapes=[
            pltpu.VMEM((3, half, 3 * inner), jnp.bfloat16),
            pltpu.VMEM((3, inner, 3 * half), jnp.bfloat16),
        ],
        compiler_params=pltpu.CompilerParams(vmem_limit_bytes=LIMIT),
        cost_estimate=pl.CostEstimate(
            flops=54 * inner * half * half, bytes_accessed=32 * inner * half, transcendentals=half * half
        ),
    )(o, w, gap_o, gap_w, *old)


def moved_from(route, by_x, by_z, count_x, count_z):
    out = {}
    for k, target in route.items():
        kx, kz = divmod(k, count_z)
        out[(kx + by_x) % count_x * count_z + (kz + by_z) % count_z] = target
    return out


def choose_kernel(turned, if_lower, if_upper, first, second, sems):
    half = first.shape[2]
    upper = on_upper()

    def copies(source, turned):
        at = [pl.ds(i * half, half) for i in ((1, 0) if turned else (0, 1))]
        return (
            pltpu.make_async_copy(source.at[:, :, at[0]], first, sems.at[0]),
            pltpu.make_async_copy(source.at[:, :, at[1]], second, sems.at[1]),
        )

    @pl.when(upper)
    def _():
        for copy in copies(if_upper, turned):
            copy.start()

    @pl.when(jnp.logical_not(upper))
    def _():
        for copy in copies(if_lower, False):
            copy.start()

    for copy in copies(if_lower, False):
        copy.wait()


def choose(if_lower, if_upper, turned):
    parts, inner, pairs = if_lower.shape
    spec = pl.BlockSpec(memory_space=pltpu.VMEM)
    return pl.pallas_call(
        functools.partial(choose_kernel, turned),
        out_shape=(jax.ShapeDtypeStruct((parts, inner, pairs // 2), if_lower.dtype),) * 2,
        in_specs=[pl.BlockSpec(memory_space=pl.ANY)] * 2,
        out_specs=(spec, spec),
        scratch_shapes=[pltpu.SemaphoreType.DMA((2,))],
        compiler_params=pltpu.CompilerParams(vmem_limit_bytes=LIMIT),
        cost_estimate=pl.CostEstimate(flops=0, bytes_accessed=8 * if_lower.size, transcendentals=0),
    )(if_lower, if_upper)


def gap_kernel(vir_a, vir_b, occ_a, occ_b, first_o, second_o, first_w, second_w):
    upper = on_upper()
    occ_o = jnp.where(upper, occ_b[...], occ_a[...])
    occ_w = jnp.where(upper, occ_a[...], occ_b[...])
    vir_o = jnp.where(upper, vir_b[...], vir_a[...])
    vir_w = jnp.where(upper, vir_a[...], vir_b[...])
    span = vir_o.shape[1]
    vir_o = jnp.broadcast_to(vir_o, (8, span)).T[:, :1]
    each = first_o.shape[0] // span
    for i in range(each):
        lower_occ, upper_occ = occ_o[:, i : i + 1], occ_o[:, each + i : each + i + 1]
        at = pl.ds(i * span, span)
        first_o[at, :] = vir_o - jnp.where(upper, upper_occ, lower_occ)
        second_o[at, :] = vir_o - jnp.where(upper, lower_occ, upper_occ)
        first_w[:, at] = vir_w - occ_w[:, i : i + 1]
        second_w[:, at] = vir_w - occ_w[:, each + i : each + i + 1]


def gaps(vir_a, vir_b, occ_a, occ_b):
    half = vir_a.shape[1] * occ_a.shape[1] // 2
    spec = pl.BlockSpec(memory_space=pltpu.VMEM)
    column = jax.ShapeDtypeStruct((half, 1), vir_a.dtype)
    row = jax.ShapeDtypeStruct((1, half), vir_a.dtype)
    out = pl.pallas_call(
        gap_kernel,
        out_shape=(column, column, row, row),
        in_specs=[spec] * 4,
        out_specs=(spec,) * 4,
        compiler_params=pltpu.CompilerParams(vmem_limit_bytes=LIMIT),
    )(vir_a, vir_b, occ_a, occ_b)
    return out[:2], out[2:]


def merge_kernel(to_a, met, re, im, for_a, for_b):
    upper = on_upper()
    for i, other in enumerate((re[...], im[...])):
        own = to_a[i] + met[i]
        for_a[i] = jnp.where(upper, other, own)
        for_b[i] = jnp.where(upper, own, other)


def merge(to_a, met, re, im):
    spec = pl.BlockSpec(memory_space=pltpu.VMEM)
    return pl.pallas_call(
        merge_kernel,
        out_shape=(jax.ShapeDtypeStruct(to_a.shape, to_a.dtype),) * 2,
        in_specs=[spec] * 4,
        out_specs=(spec, spec),
        compiler_params=pltpu.CompilerParams(vmem_limit_bytes=LIMIT),
    )(to_a, met, re, im)


def finish_kernel(early, lowered, back_a, back_b, hop_re, hop_im, back_re, back_im, out, held, sems):
    half = back_a.shape[2]
    steps = sems.shape[0]
    rows = back_a.shape[1] // steps
    upper = on_upper()
    copies = []
    for i in range(steps):
        at = pl.ds(i * rows, rows)
        a, b = back_a[:, at], back_b[:, at]
        held[:, at, :half] = -jnp.where(upper, a, early[:, at] + lowered[:, at])
        even = a + b
        held[0, at, half:] = -jnp.where(upper, b[0], even[0] + hop_re[at] + back_re[at])
        held[1, at, half:] = -jnp.where(upper, b[1], even[1] + hop_im[at] + back_im[at])
        copies.append(pltpu.make_async_copy(held.at[:, at], out.at[:, at], sems.at[i]))
        copies[-1].start()
    for copy in copies:
        copy.wait()


def finish(*backs):
    parts, inner, half = backs[0].shape
    shape = (parts, inner, 2 * half)
    return pl.pallas_call(
        finish_kernel,
        out_shape=jax.ShapeDtypeStruct(shape, backs[0].dtype),
        in_specs=[pl.BlockSpec(memory_space=pltpu.VMEM)] * 8,
        out_specs=pl.BlockSpec(memory_space=pl.ANY),
        scratch_shapes=[pltpu.VMEM(shape, backs[0].dtype), pltpu.SemaphoreType.DMA((6,))],
        compiler_params=pltpu.CompilerParams(vmem_limit_bytes=LIMIT),
    )(*backs)


def body(factors, occ_energy, vir_energy, shifts):
    count_x, count_z = lax.axis_size("kxy"), lax.axis_size("kz")
    odd, after, before = routes(count_x, count_z)
    route_a = {**onto(odd, 0), **onto(after, 1)}
    route_b = {**onto(odd, 1), **onto(before, 0)}
    route_after = onto(after, 1)
    route_before = onto(before, 0)
    cores = {i: i ^ count_z for i in range(count_x * count_z)}
    route_early = {t: s for s, t in route_after.items()} | {t: s ^ count_z for s, t in route_before.items()}
    first_after, second_after, homes_after = around(after, 1, AROUND_AFTER, count_z)
    first_before, second_before, homes_before = around(before, 0, AROUND_BEFORE, count_z)
    first_hop = {**first_after, **first_before}
    second_hop = {**second_after, **second_before}
    part_after, leave_after, parted_after = around(after, 1, PARTED_AFTER, count_z)
    part_before, leave_before, parted_before = around(before, 0, PARTED_BEFORE, count_z)
    part_hop = {**part_after, **part_before}
    leave_hop = {**leave_after, **leave_before}
    straight = {route_after[s]: s for s in parted_after} | {route_before[s]: s for s in parted_before}
    not_a, not_b = homes_after | parted_after, homes_before | parted_before
    late_a = {**onto(odd, 0), **{s: t for s, t in route_after.items() if s not in not_a}}
    late_b = {**onto(odd, 1), **{s: t for s, t in route_before.items() if s not in not_b}}
    downward = {s: t for s, t in cores.items() if s > t}
    upward = {s: t for s, t in cores.items() if s < t}

    own = factors[0, 0]
    arrived_a = move(own, route_a)
    arrived_b = move(own, route_before)

    occ_a = move(occ_energy[0], route_a)
    occ_b = move(occ_energy[0], route_b)

    def send_energies(by_x, by_z):
        def send(vir):
            return tuple(
                move(vir, moved_from(route, by_x, by_z, count_x, count_z)) for route in (route_a, route_b)
            )

        return send

    span = REACH - 1
    sends = [send_energies(1 + i // span, 1 + i % span) for i in range(span * span)]
    vir_a, vir_b = lax.switch((shifts[0, 0] - 1) * span + shifts[0, 1] - 1, sends, vir_energy[0])
    arrived_a, vir_a, vir_b = lax.optimization_barrier((arrived_a, vir_a, vir_b))
    crossed = move(arrived_a, upward)
    w = choose(arrived_b, arrived_a, False)
    gap_o, gap_w = gaps(vir_a, vir_b, occ_a, occ_b)
    o = choose(arrived_a, crossed, True)

    to_a, to_f = block(o[0], w[0], gap_o[0], gap_w[0])
    to_b, to_f = block(o[1], w[0], gap_o[1], gap_w[0], old_w=to_f)
    back_early = move(to_f, route_early)
    to_b, to_s = block(o[1], w[1], gap_o[1], gap_w[1], old_o=to_b)
    met = move(to_b, cores)
    to_a, re, im = block(o[0], w[1], gap_o[0], gap_w[1], to_a, to_s, parted=True)
    middle_re = move(re, first_hop | part_hop)
    middle_im = move(im, first_hop)
    for_a, for_b = merge(to_a, met, re, im)
    back_a = move_back(for_a, late_a)
    back_b = move_back(for_b, late_b)
    back_im = move(im, straight)
    hop_re = move(middle_re, second_hop)
    back_re = move(middle_re, leave_hop)
    hop_im = move(middle_im, second_hop)
    lowered = move(back_early, downward)
    return finish(back_early, lowered, back_a, back_b, hop_re, hop_im, back_re, back_im)[None, None]


def solution(mesh):
    placed = (P("kxy", "kz", None, None, None), P("kxy", "kz", None), P("kxy", "kz", None), P())
    return jax.shard_map(
        body,
        mesh=mesh,
        in_specs=placed,
        out_specs=P("kxy", "kz", None, None, None),
        check_vma=False,
    )
```
